32 devices in a mesh: cores: 4 (over y, x), row: 4 (over z), tensor: 2 (over core).
Axes of the slice: x: 2, y: 2, z: 4, core: 2. Of those that a mesh axis runs over, the one named last changes fastest.
Arguments:
- cores: float32 [2, 4, 128, 256, 256], P('tensor', 'cores', 'row'), may hold values from -1 to 1, as said below
- incoming: float32 [2, 256, 256], P('tensor'), may hold values from -1 to 2, as said below
Outputs:
- frames: float32 [2, 4, 128, 256, 256], P('tensor', 'cores', 'row')
- tail: float32 [2, 256, 256], P('tensor', 'cores')
- correlation: float32 [2, 256, 256], P('tensor', 'cores')
The draws below stay inside these ranges and needn't reach their ends.
Inputs may be any that keep to these rules, and one draw needn't show every extreme that they name: `cores`: each core's unfolding over (mode index, left rank) has full column rank and is well conditioned. `incoming`: upper triangular, diagonal entries from 1 to 2.
All inputs are finite; a program needn't handle non-finite values.
Results may differ from the reference program's by a relative error of at most 0.0001.
Values sent between devices are 32-bit elements; how exact they have to be, the bound alone decides.
A program may use at most 192 MiB of HBM per device.

```python
import jax
import jax.numpy as jnp
from jax import lax

RANK = 256
MODE = 128
TRAIN_CORES = 4


def draw_cores(key, part):
    shape = (TRAIN_CORES, MODE, RANK, RANK)
    common = jax.random.normal(jax.random.fold_in(key, 11), (1,) + shape, jnp.float32)
    noise = jax.random.normal(jax.random.fold_in(key, 12), (2,) + shape, jnp.float32)
    mixed_gram = common + 0.3 * noise
    return mixed_gram / jnp.sqrt(1.09 * MODE * RANK)


def draw_incoming(key, part):
    diagonal = jax.random.uniform(jax.random.fold_in(key, 21), (2, RANK), jnp.float32, 1.0, 2.0)
    spread = jax.random.normal(jax.random.fold_in(key, 22), (2, RANK, RANK), jnp.float32) * (0.8 / RANK ** 0.5)
    spread = jnp.clip(spread, -0.9, 0.9)
    strict = jnp.triu(spread, 1)
    return strict + jax.vmap(jnp.diag)(diagonal)


def setup_inputs(seed: int = 0) -> dict:
    arg_keys = jax.random.split(jax.random.key(seed), 3)
    return {
        "cores": draw_cores(jax.random.fold_in(arg_keys[2], 71), 0),
        "incoming": draw_incoming(jax.random.fold_in(arg_keys[2], 71), 0),
    }


HIGH_PRECISION = lax.Precision.HIGHEST

def chain_step(upper, block):
    mixed_gram = jnp.einsum('ab,ibc->iac', upper, block, precision=HIGH_PRECISION)
    gram_matrix = jnp.einsum('bgk,bgj->kj', mixed_gram, mixed_gram, precision=HIGH_PRECISION)
    lower = jnp.linalg.cholesky(gram_matrix)
    identity_matrix = jnp.eye(gram_matrix.shape[0], dtype=gram_matrix.dtype)
    inverse_factor = lax.linalg.triangular_solve(lower, identity_matrix, left_side=True, lower=True)
    basis_frame = jnp.einsum('pwv,kv->pwk', mixed_gram, inverse_factor, precision=HIGH_PRECISION)
    return (basis_frame, lower.T)

def link_step(link, left, right):
    middle = jnp.einsum('bc,icd->ibd', link, right, precision=HIGH_PRECISION)
    return jnp.einsum('iba,ibd->ad', left, middle, precision=HIGH_PRECISION)

def reference(cores, incoming):
    factor = float(MODE * RANK) ** 0.5
    frame_list = []
    tails = []
    correlations = []
    for which in range(2):
        upper = incoming[which]
        blocks = []
        for index in range(TRAIN_CORES):
            basis_frame, upper = chain_step(upper, cores[which, index])
            blocks.append(basis_frame * factor)
        frame_list.append(jnp.stack(blocks))
        tails.append(upper)
        other = 1 - which
        link = jnp.dot(incoming[which].T, incoming[other], precision=HIGH_PRECISION)
        for index in range(TRAIN_CORES):
            link = link_step(link, cores[which, index], cores[other, index])
        correlations.append(link)
    return (jnp.stack(frame_list), jnp.stack(tails), jnp.stack(correlations))
```

```python
import functools

import jax
import jax.numpy as jnp
from jax import lax
from jax.experimental import pallas as pl
from jax.experimental.pallas import tpu as pltpu
from jax.sharding import PartitionSpec as P

MESH = pl.DeviceIdType.MESH
F32 = jnp.float32
BF16 = jnp.bfloat16
NEWTON_STEPS = 7


def split(x):
    hi = x.astype(BF16)
    return hi, (x - hi.astype(F32)).astype(BF16)


def left3(hi, lo):
    return jnp.concatenate([hi, hi, lo], axis=1)


def right3(hi, lo):
    return jnp.concatenate([hi, lo, hi], axis=0)


def right3t(hi, lo):
    return jnp.concatenate([hi, lo, hi], axis=1)


def dot(a, b):
    return jnp.dot(a, b, preferred_element_type=F32)


def dot_nt(a, b):
    return lax.dot_general(a, b, (((1,), (1,)), ((), ())), preferred_element_type=F32)


def mm(a, b):
    return dot(left3(*split(a)), right3(*split(b)))


def mm_nt(a, b):
    return dot_nt(left3(*split(a)), right3t(*split(b)))


def chain_kernel(
    S, R, group,
    cores_ref, incoming_ref,
    gin_out, gout_out, gfin_out, lfin_out,
    raw, other, in_other, c_hi, c_lo, ct_hi, ct_lo, o_hi, o_lo,
    gin, gout, gfin, lin, lfin, p_ref, q_ref, rs_p, rs_q, red_p, red_q, acc,
    raw_sem, pair_send, pair_recv,
    rsp_send, rsp_recv, rsq_send, rsq_recv,
    hop_send, hop_recv, lhop_send, lhop_recv,
    fout_send, fout_recv, ffin_send, ffin_recv, flin_send, flin_recv,
    gf_send, gf_recv, lf_send, lf_recv,
):
    s = lax.axis_index("cores")
    r = lax.axis_index("row")
    t = lax.axis_index("tensor")
    modes, n, _ = raw.shape
    half = modes // 2
    ch = n // R
    wide = n // 2

    def row_at(d):
        return lax.rem(r + d, R)

    def tens(e):
        return lax.rem(t + e, 2)

    def rows(k):
        return pl.ds(pl.multiple_of(k * ch, ch), ch)

    def cols(k):
        return pl.ds(pl.multiple_of(k * wide, wide), wide)

    barrier = pltpu.get_barrier_semaphore()
    greeted = 0
    for d in range(R):
        for e in range(2):
            for q in range(S):
                if d == 0 and e == 0 and q == 0:
                    continue
                if q > 0 and e > 0 and q != 1 and q != S - 1:
                    continue
                pl.semaphore_signal(
                    barrier, inc=1, device_id=(lax.rem(s + q, S), row_at(d), tens(e)), device_id_type=MESH
                )
                greeted += 1
    pl.semaphore_wait(barrier, greeted)

    def remote(src, dst, send, recv, to):
        return pltpu.make_async_remote_copy(
            src_ref=src, dst_ref=dst, send_sem=send, recv_sem=recv, device_id=to, device_id_type=MESH
        )

    partner = (s, r, tens(1))
    give = remote(cores_ref.at[pl.ds((1 - t) * half, half)], other, pair_send.at[0], pair_recv.at[0], partner)
    give_in = remote(incoming_ref, in_other, pair_send.at[1], pair_recv.at[1], partner)
    give_in.start()
    give.start()

    groups = modes // group
    loads = [
        pltpu.make_async_copy(cores_ref.at[pl.ds(k * group, group)], raw.at[pl.ds(k * group, group)], raw_sem.at[k])
        for k in range(groups)
    ]
    for load in loads:
        load.start()
    for k in range(groups):
        loads[k].wait()

        def prep(j, carry, k=k):
            i = k * group + j
            x = raw[i]
            hi, lo = split(x)
            c_hi[i] = hi
            c_lo[i] = lo
            thi, tlo = split(x.T)
            ct_hi[i] = thi
            ct_lo[i] = tlo
            return carry

        lax.fori_loop(0, group, prep, 0)

    def prep_other():
        give.wait()
        give_in.wait()

        def body(j, carry):
            hi, lo = split(other[j])
            o_hi[j] = hi
            o_lo[j] = lo
            return carry

        lax.fori_loop(0, half, body, 0)

    nxt = lax.rem(s + 1, S)

    def g_hop(d):
        return remote(red_p, gin.at[rows(r)], hop_send.at[d], hop_recv.at[d], (nxt, row_at(d), t))

    def l_hop(d, e):
        return remote(
            red_q, lin.at[rows(r), cols(t)], lhop_send.at[d, e], lhop_recv.at[d, e], (nxt, row_at(d), tens(e))
        )

    pairs = [(d, e) for d in range(R) for e in range(2)]
    others = pairs[1:]

    @pl.when(s == 0)
    def _():
        u = incoming_ref[...]
        gin[...] = mm(u.T, u)

    @pl.when(s > 0)
    def _():
        prep_other()
        for d in range(R):
            g_hop(d).wait_recv()

    def run(w_ref, hi_ref, lo_ref, first, count, transpose):
        w = w_ref[...]
        w3 = left3(*split(w.T if transpose else w))
        acc[...] = jnp.zeros_like(acc)

        def body(k, carry):
            lhs = []
            rhs = []
            for j in range(group):
                i = k * group + j
                y = dot(w3, right3(hi_ref[i], lo_ref[i]))
                rhs.append(right3(*split(y)))
                lhs.append(left3(ct_hi[first + i], ct_lo[first + i]))
            acc[...] += dot(jnp.concatenate(lhs, axis=1), jnp.concatenate(rhs, axis=0))
            return carry

        lax.fori_loop(0, count // group, body, 0)

    run(gin, c_hi, c_lo, 0, modes, False)
    p_ref[...] = acc[...]

    def rsp(d):
        return remote(p_ref.at[rows(row_at(d))], rs_p.at[d], rsp_send.at[d], rsp_recv.at[d], (s, row_at(d), t))

    for d in range(1, R):
        rsp(d).start()

    @pl.when(s == 0)
    def _():
        prep_other()
        u = incoming_ref[...]
        v = in_other[...]

        @pl.when(t == 0)
        def _():
            lin[...] = mm(u.T, v)

        @pl.when(t == 1)
        def _():
            lin[...] = mm(v.T, u)

    @pl.when(s > 0)
    def _():
        for d, e in pairs:
            l_hop(d, e).wait_recv()

    first = t * half

    @pl.when(t == 0)
    def _():
        run(lin, o_hi, o_lo, first, half, False)
        q_ref[...] = acc[...]

    @pl.when(t == 1)
    def _():
        run(lin, o_hi, o_lo, first, half, True)
        q_ref[...] = acc[...].T

    for d in range(1, R):
        rsp(d).wait_recv()
    total = p_ref[rows(r), :]
    for d in range(1, R):
        total += rs_p[d]
    red_p[...] = total
    gout[rows(r), :] = total

    def g_fin(q):
        return remote(red_p, gfin.at[rows(r)], gf_send.at[q], gf_recv.at[0], (lax.rem(s + q, S), r, t))

    @pl.when(s < S - 1)
    def _():
        for d in range(R):
            g_hop(d).start()

    @pl.when(s == S - 1)
    def _():
        gfin[rows(r), :] = red_p[...]
        for q in range(1, S):
            g_fin(q).start()

    def rsq(d, e):
        return remote(
            q_ref.at[rows(row_at(d)), cols(tens(e))], rs_q.at[d, e], rsq_send.at[d, e], rsq_recv.at[d, e],
            (s, row_at(d), tens(e)),
        )

    for d, e in others:
        rsq(d, e).start()
    for d, e in others:
        rsq(d, e).wait_recv()
    total = q_ref[rows(r), cols(t)]
    for d, e in others:
        total += rs_q[d, e]
    red_q[...] = total

    def l_fin(q):
        return remote(red_q, lfin.at[rows(r), cols(t)], lf_send.at[q], lf_recv.at[0], (lax.rem(s + q, S), r, t))

    @pl.when(s < S - 1)
    def _():
        for d, e in pairs:
            l_hop(d, e).start()

    @pl.when(s == S - 1)
    def _():
        lfin[rows(r), cols(t)] = red_q[...]
        for q in range(1, S):
            l_fin(q).start()

    def fan(buf, send, recv, d):
        return remote(buf.at[rows(r)], buf.at[rows(r)], send.at[d], recv.at[d], (s, row_at(d), t))

    def fan_l(d, e):
        return remote(
            lfin.at[rows(r), cols(t)], lfin.at[rows(r), cols(t)], flin_send.at[d, e], flin_recv.at[d, e],
            (s, row_at(d), tens(e)),
        )

    for d in range(1, R):
        fan(gout, fout_send, fout_recv, d).start()

    @pl.when(s < S - 1)
    def _():
        g_fin(0).wait_recv()

    for d in range(1, R):
        fan(gfin, ffin_send, ffin_recv, d).start()

    @pl.when(s < S - 1)
    def _():
        l_fin(0).wait_recv()

    for d, e in others:
        fan_l(d, e).start()

    for d in range(1, R):
        fan(gout, fout_send, fout_recv, d).wait_recv()
        fan(gfin, ffin_send, ffin_recv, d).wait_recv()
    for d, e in others:
        fan_l(d, e).wait_recv()
    gin_out[...] = gin[...]
    gout_out[...] = gout[...]
    gfin_out[...] = gfin[...]
    lfin_out[...] = lfin[...]
    for d in range(1, R):
        rsp(d).wait_send()
        fan(gout, fout_send, fout_recv, d).wait_send()
        fan(gfin, ffin_send, ffin_recv, d).wait_send()
    for d, e in others:
        rsq(d, e).wait_send()
        fan_l(d, e).wait_send()

    @pl.when(s < S - 1)
    def _():
        for d in range(R):
            g_hop(d).wait_send()
        for d, e in pairs:
            l_hop(d, e).wait_send()

    @pl.when(s == S - 1)
    def _():
        for q in range(1, S):
            g_fin(q).wait_send()
            l_fin(q).wait_send()


def chain(block, incoming, S, R):
    modes, n, _ = block.shape
    half = modes // 2
    group = 1
    while group < 4 and half % (2 * group) == 0:
        group *= 2
    ch = n // R
    dma = pltpu.SemaphoreType.DMA
    vmem = pltpu.VMEM
    full = jax.ShapeDtypeStruct((n, n), F32)
    return pl.pallas_call(
        functools.partial(chain_kernel, S, R, group),
        out_shape=[full] * 4,
        in_specs=[pl.BlockSpec(memory_space=pl.ANY), pl.BlockSpec(memory_space=pltpu.VMEM)],
        out_specs=[pl.BlockSpec(memory_space=pltpu.VMEM)] * 4,
        scratch_shapes=[
            vmem((modes, n, n), F32), vmem((half, n, n), F32), vmem((n, n), F32),
            vmem((modes, n, n), BF16), vmem((modes, n, n), BF16),
            vmem((modes, n, n), BF16), vmem((modes, n, n), BF16),
            vmem((half, n, n), BF16), vmem((half, n, n), BF16),
            vmem((n, n), F32), vmem((n, n), F32), vmem((n, n), F32), vmem((n, n), F32), vmem((n, n), F32),
            vmem((n, n), F32), vmem((n, n), F32),
            vmem((R, ch, n), F32), vmem((R, 2, ch, n // 2), F32),
            vmem((ch, n), F32), vmem((ch, n // 2), F32), vmem((n, n), F32),
            dma((modes // group,)), dma((2,)), dma((2,)),
            dma((R,)), dma((R,)), dma((R, 2)), dma((R, 2)),
            dma((R,)), dma((R,)), dma((R, 2)), dma((R, 2)),
            dma((R,)), dma((R,)), dma((R,)), dma((R,)), dma((R, 2)), dma((R, 2)),
            dma((S,)), dma((1,)), dma((S,)), dma((1,)),
        ],
        compiler_params=pltpu.CompilerParams(
            collective_id=0, has_side_effects=True, vmem_limit_bytes=60 * 1024 * 1024
        ),
        name="gram_chain",
    )(block, incoming)


def lower_part(e):
    row = lax.broadcasted_iota(jnp.int32, e.shape, 0)
    col = lax.broadcasted_iota(jnp.int32, e.shape, 1)
    return jnp.where(row > col, e, jnp.where(row == col, 0.5 * e, 0.0))


def frame_kernel(
    group, scale, g_ref, incoming_ref, blocks_ref, frames_ref, tail_ref, x_ref, a_ref, b_ref, u_hi, u_lo, x_hi, x_lo
):
    n = incoming_ref.shape[0]
    count = g_ref.shape[0]
    section = lax.axis_index("cores")
    sections = lax.axis_size("cores")

    @pl.when(pl.program_id(0) == 0)
    def _():
        row = lax.broadcasted_iota(jnp.int32, (n, n), 0)
        col = lax.broadcasted_iota(jnp.int32, (n, n), 1)
        eye = (row == col).astype(F32)
        for m in range(count):
            diagonal = jnp.sum(g_ref[m] * eye, axis=0, keepdims=True)
            x_ref[m] = eye * lax.rsqrt(diagonal)

        def residual(m):
            x = x_ref[m]
            return x, mm_nt(mm(x, g_ref[m]), x) - eye

        def step(k, carry):
            for m in range(count):
                x, e = residual(m)
                x_ref[m] = x - mm(lower_part(e), x)
            return carry

        lax.fori_loop(0, NEWTON_STEPS, step, 0)

        for m in range(count):
            x, e = residual(m)
            distance = jnp.sum(e * e)
            smallest = jnp.min(jnp.where(row == col, x, 1.0))

            @pl.when(jnp.logical_not((distance < 1e-6) & (smallest > 0.0)))
            def _(m=m):
                a_ref[...] = g_ref[m]
                b_ref[...] = eye

                def column(j, carry):
                    a = a_ref[...]
                    b = b_ref[...]
                    rowj = jnp.sum(jnp.where(row == j, a, 0.0), axis=0, keepdims=True)
                    pivot = jnp.sum(jnp.where((row == j) & (col == j), a, 0.0), keepdims=True)
                    inv = lax.rsqrt(pivot)
                    colj = jnp.sum(jnp.where(col == j, a, 0.0), axis=1, keepdims=True) * inv
                    below = lax.broadcasted_iota(jnp.int32, (n, 1), 0) > j
                    colj = jnp.where(below, colj, 0.0)
                    bj = jnp.sum(jnp.where(row == j, b, 0.0), axis=0, keepdims=True) * inv
                    a_ref[...] = a - colj * (rowj * inv)
                    b_ref[...] = jnp.where(row == j, bj, b) - colj * bj
                    return carry

                lax.fori_loop(0, n, column, 0)
                x_ref[m] = b_ref[...]

        def factor(m):
            return jnp.where(row <= col, mm(x_ref[m], g_ref[m]), 0.0)

        tail_ref[...] = factor(2)
        upper = jnp.where(section == 0, incoming_ref[...], factor(0))
        hi, lo = split(upper)
        u_hi[...] = hi
        u_lo[...] = lo
        hi, lo = split(jnp.where(row >= col, x_ref[1], 0.0).T * scale)
        x_hi[...] = hi
        x_lo[...] = lo

    u3 = left3(u_hi[...], u_lo[...])
    x3 = right3(x_hi[...], x_lo[...])
    for j in range(group):
        mixed = dot(u3, right3(*split(blocks_ref[j])))
        frames_ref[j] = dot(left3(*split(mixed)), x3)


def make_frames(grams, incoming, block, scale):
    modes, n, _ = block.shape
    group = min(4, modes)
    vmem = pltpu.VMEM
    return pl.pallas_call(
        functools.partial(frame_kernel, group, scale),
        grid=(modes // group,),
        out_shape=[jax.ShapeDtypeStruct((modes, n, n), F32), jax.ShapeDtypeStruct((n, n), F32)],
        in_specs=[
            pl.BlockSpec((3, n, n), lambda i: (0, 0, 0)),
            pl.BlockSpec((n, n), lambda i: (0, 0)),
            pl.BlockSpec((group, n, n), lambda i: (i, 0, 0)),
        ],
        out_specs=[
            pl.BlockSpec((group, n, n), lambda i: (i, 0, 0)),
            pl.BlockSpec((n, n), lambda i: (0, 0)),
        ],
        scratch_shapes=[
            vmem((3, n, n), F32), vmem((n, n), F32), vmem((n, n), F32),
            vmem((n, n), BF16), vmem((n, n), BF16), vmem((n, n), BF16), vmem((n, n), BF16),
        ],
        compiler_params=pltpu.CompilerParams(vmem_limit_bytes=48 * 1024 * 1024),
        name="frames",
    )(grams, incoming, block)


def shards(S, R, T, modes_all, cores, incoming):
    block = cores[0, 0]
    upper_start = incoming[0]
    n = block.shape[-1]
    section = lax.axis_index("cores")
    tensor = lax.axis_index("tensor")
    gin, gout, gfin, link = chain(block, upper_start, S, R)
    gin = jnp.where(section == 0, jnp.eye(n, dtype=F32), gin)
    gout = jnp.where(section == S - 1, gfin, gout)
    scale = float(modes_all * n) ** 0.5
    frames, tail = make_frames(jnp.stack([gin, gout, gfin]), upper_start, block, scale)
    share = n // S
    link = jnp.where(tensor == 0, link, link.T)
    tail_rows = lax.dynamic_slice_in_dim(tail, section * share, share, 0)
    link_rows = lax.dynamic_slice_in_dim(link, section * share, share, 0)
    return frames[None, None], tail_rows[None], link_rows[None]


def solution(mesh):
    S, R, T = (mesh.shape[name] for name in ("cores", "row", "tensor"))
    in_specs = (P("tensor", "cores", "row", None, None), P("tensor", None, None))
    out_specs = (
        P("tensor", "cores", "row", None, None),
        P("tensor", "cores", None),
        P("tensor", "cores", None),
    )

    def whole(cores, incoming):
        body = functools.partial(shards, S, R, T, cores.shape[2])
        return jax.shard_map(body, mesh=mesh, in_specs=in_specs, out_specs=out_specs, check_vma=False)(
            cores, incoming
        )

    return whole
```

```python
import functools

import jax
import jax.numpy as jnp
from jax import lax
from jax.experimental import pallas as pl
from jax.experimental.pallas import tpu as pltpu
from jax.sharding import PartitionSpec as P

MESH = pl.DeviceIdType.MESH
F32 = jnp.float32
BF16 = jnp.bfloat16
NEWTON_STEPS = 16
CLOSE = 1e-6


def split(x):
    hi = x.astype(BF16)
    return hi, (x - hi.astype(F32)).astype(BF16)


def left3(hi, lo):
    return jnp.concatenate([hi, hi, lo], axis=1)


def right3(hi, lo):
    return jnp.concatenate([hi, lo, hi], axis=0)


def right3t(hi, lo):
    return jnp.concatenate([hi, lo, hi], axis=1)


def dot(a, b):
    return jnp.dot(a, b, preferred_element_type=F32)


def dot_nt(a, b):
    return lax.dot_general(a, b, (((1,), (1,)), ((), ())), preferred_element_type=F32)


def mm(a, b):
    return dot(left3(*split(a)), right3(*split(b)))


def mm_nt(a, b):
    return dot_nt(left3(*split(a)), right3t(*split(b)))


def pack(g, blocks):
    h = g.shape[0] // 2
    parts = [g[:h, :h], g[:h, h:], g[h:, h:]]
    if blocks == 4:
        parts.append(g[h:, :h])
    return jnp.concatenate(parts, axis=0)


def unpack(p):
    h = p.shape[1]
    a, b, c = p[:h], p[h : 2 * h], p[2 * h : 3 * h]
    return jnp.concatenate(
        [jnp.concatenate([a, b], axis=1), jnp.concatenate([b.T, c], axis=1)], axis=0
    )


def chain_kernel(
    S, R, group, blocks,
    cores_ref, incoming_ref,
    grams_out, link_out,
    raw, other, in_other, c_hi, c_lo, ct_hi, ct_lo, o_hi, o_lo,
    gin, gout, gfin, lin, lfin, p_ref, q_ref, q_got, q_sum, rs_p, rs_q, red_p, red_q, acc, turned,
    raw_sem, pair_send, pair_recv,
    rsp_send, rsp_recv, rsq_send, rsq_recv, swap_send, swap_recv, half_send, half_recv,
    hop_send, hop_recv, lhop_send, lhop_recv,
    fout_send, fout_recv, ffin_send, ffin_recv, flin_send, flin_recv,
    gf_send, gf_recv, lf_send, lf_recv,
):
    s = lax.axis_index("cores")
    r = lax.axis_index("row")
    t = lax.axis_index("tensor")
    modes, n, _ = raw.shape
    half = modes // 2
    ch = n // R
    wide = n // 2

    def row_at(d):
        return lax.rem(r + d, R)

    def tens(e):
        return lax.rem(t + e, 2)

    part = blocks * wide // R

    def rows(k):
        return pl.ds(pl.multiple_of(k * ch, ch), ch)

    def parts(k):
        return pl.ds(pl.multiple_of(k * part, part), part)

    def cols(k):
        return pl.ds(pl.multiple_of(k * wide, wide), wide)

    barrier = pltpu.get_barrier_semaphore()
    greeted = 0
    for d in range(R):
        for e in range(2):
            for q in range(S):
                if d == 0 and e == 0 and q == 0:
                    continue
                if q > 0 and e > 0:
                    continue
                pl.semaphore_signal(
                    barrier, inc=1, device_id=(lax.rem(s + q, S), row_at(d), tens(e)), device_id_type=MESH
                )
                greeted += 1
    pl.semaphore_wait(barrier, greeted)

    def remote(src, dst, send, recv, to):
        return pltpu.make_async_remote_copy(
            src_ref=src, dst_ref=dst, send_sem=send, recv_sem=recv, device_id=to, device_id_type=MESH
        )

    partner = (s, r, tens(1))
    give = remote(cores_ref.at[pl.ds((1 - t) * half, half)], other, pair_send.at[0], pair_recv.at[0], partner)
    give_in = remote(incoming_ref, in_other, pair_send.at[1], pair_recv.at[1], partner)
    give_in.start()
    give.start()

    groups = modes // group
    loads = [
        pltpu.make_async_copy(cores_ref.at[pl.ds(k * group, group)], raw.at[pl.ds(k * group, group)], raw_sem.at[k])
        for k in range(groups)
    ]
    for load in loads:
        load.start()
    for k in range(groups):
        loads[k].wait()

        def prep(j, carry, k=k):
            i = k * group + j
            x = raw[i]
            hi, lo = split(x)
            c_hi[i] = hi
            c_lo[i] = lo
            thi, tlo = split(x.T)
            ct_hi[i] = thi
            ct_lo[i] = tlo
            return carry

        lax.fori_loop(0, group, prep, 0)

    def prep_other():
        give.wait()
        give_in.wait()

        def body(j, carry):
            hi, lo = split(other[j])
            o_hi[j] = hi
            o_lo[j] = lo
            return carry

        lax.fori_loop(0, half, body, 0)

    nxt = lax.rem(s + 1, S)

    def g_hop(d):
        return remote(red_p, gin.at[parts(r)], hop_send.at[d], hop_recv.at[d], (nxt, row_at(d), t))

    def l_hop(d):
        return remote(red_q, lin.at[t, rows(r)], lhop_send.at[d], lhop_recv.at[d], (nxt, row_at(d), t))

    def l_half():
        return remote(lin.at[t], lin.at[t], half_send, half_recv, partner)

    pairs = [(d, e) for d in range(R) for e in range(2)]
    others = pairs[1:]

    @pl.when(s == 0)
    def _():
        u = incoming_ref[...]
        gin[...] = pack(mm(u.T, u), blocks)

    @pl.when(s > 0)
    def _():
        prep_other()
        for d in range(R):
            g_hop(d).wait_recv()

    def run(w, hi_ref, lo_ref, first, count):
        w3 = left3(*split(w))
        acc[...] = jnp.zeros_like(acc)

        def body(k, carry):
            lhs = []
            rhs = []
            for j in range(group):
                i = k * group + j
                y = dot(w3, right3(hi_ref[i], lo_ref[i]))
                rhs.append(right3(*split(y)))
                lhs.append(left3(ct_hi[first + i], ct_lo[first + i]))
            acc[...] += dot(jnp.concatenate(lhs, axis=1), jnp.concatenate(rhs, axis=0))
            return carry

        lax.fori_loop(0, count // group, body, 0)

    run(unpack(gin[...]), c_hi, c_lo, 0, modes)
    p_ref[...] = pack(acc[...], blocks)

    def rsp(d):
        return remote(p_ref.at[parts(row_at(d))], rs_p.at[d], rsp_send.at[d], rsp_recv.at[d], (s, row_at(d), t))

    for d in range(1, R):
        rsp(d).start()

    def put(m):
        lin[0] = m[:, :wide]
        lin[1] = m[:, wide:]

    @pl.when(s == 0)
    def _():
        prep_other()
        u = incoming_ref[...]
        v = in_other[...]

        @pl.when(t == 0)
        def _():
            put(mm(u.T, v))

        @pl.when(t == 1)
        def _():
            put(mm(v.T, u))

    @pl.when(s > 0)
    def _():
        for d in range(R):
            l_hop(d).wait_recv()
        l_half().start()
        l_half().wait_recv()

    first = t * half
    link = jnp.concatenate([lin[0], lin[1]], axis=1)

    @pl.when(t == 0)
    def _():
        run(link, o_hi, o_lo, first, half)
        q_ref[0] = acc[:, :wide]
        q_ref[1] = acc[:, wide:]

    @pl.when(t == 1)
    def _():
        run(link.T, o_hi, o_lo, first, half)
        turned[...] = acc[...].T
        q_ref[0] = turned[:, :wide]
        q_ref[1] = turned[:, wide:]

    swap = remote(q_ref.at[1 - t], q_got, swap_send, swap_recv, partner)
    swap.start()

    for d in range(1, R):
        rsp(d).wait_recv()
    total = p_ref[parts(r), :]
    for d in range(1, R):
        total += rs_p[d]
    red_p[...] = total

    def g_fin(q):
        return remote(red_p, gfin.at[parts(r)], gf_send.at[q], gf_recv.at[0], (lax.rem(s + q, S), r, t))

    def fan(buf, send, recv, d):
        return remote(red_p, buf.at[parts(r)], send.at[d], recv.at[d], (s, row_at(d), t))

    def fan_fin(d):
        return remote(gfin.at[parts(r)], gfin.at[parts(r)], ffin_send.at[d], ffin_recv.at[d], (s, row_at(d), t))

    @pl.when(s < S - 1)
    def _():
        for d in range(R):
            g_hop(d).start()

    @pl.when(s == S - 1)
    def _():
        gfin[parts(r), :] = red_p[...]
        for d in range(1, R):
            fan_fin(d).start()
        for q in range(1, S):
            g_fin(q).start()

    swap.wait_recv()
    q_sum[...] = q_ref[t] + q_got[...]

    def rsq(d):
        return remote(q_sum.at[rows(row_at(d))], rs_q.at[d], rsq_send.at[d], rsq_recv.at[d], (s, row_at(d), t))

    for d in range(1, R):
        rsq(d).start()
    for d in range(1, R):
        rsq(d).wait_recv()
    total = q_sum[rows(r), :]
    for d in range(1, R):
        total += rs_q[d]
    red_q[...] = total

    def l_fin(q):
        return remote(red_q, lfin.at[t, rows(r)], lf_send.at[q], lf_recv.at[0], (lax.rem(s + q, S), r, t))

    def fan_l(d, e):
        return remote(
            lfin.at[t, rows(r)], lfin.at[t, rows(r)], flin_send.at[d, e], flin_recv.at[d, e], (s, row_at(d), tens(e))
        )

    @pl.when(s < S - 1)
    def _():
        for d in range(R):
            l_hop(d).start()
        gout[parts(r), :] = red_p[...]
        for d in range(1, R):
            fan(gout, fout_send, fout_recv, d).start()
        g_fin(0).wait_recv()
        for d in range(1, R):
            fan_fin(d).start()
        l_fin(0).wait_recv()

    @pl.when(s == S - 1)
    def _():
        lfin[t, rows(r)] = red_q[...]
        for q in range(1, S):
            l_fin(q).start()

    for d, e in others:
        fan_l(d, e).start()

    for d in range(1, R):
        fan_fin(d).wait_recv()
    final = unpack(gfin[...])
    grams_out[2] = final

    @pl.when(s == 0)
    def _():
        row = lax.broadcasted_iota(jnp.int32, (n, n), 0)
        col = lax.broadcasted_iota(jnp.int32, (n, n), 1)
        grams_out[0] = (row == col).astype(F32)

    @pl.when(s > 0)
    def _():
        grams_out[0] = unpack(gin[...])

    @pl.when(s < S - 1)
    def _():
        for d in range(1, R):
            fan(gout, fout_send, fout_recv, d).wait_recv()
        grams_out[1] = unpack(gout[...])

    @pl.when(s == S - 1)
    def _():
        grams_out[1] = final

    for d, e in others:
        fan_l(d, e).wait_recv()
    link = jnp.concatenate([lfin[0], lfin[1]], axis=1)

    @pl.when(t == 0)
    def _():
        turned[...] = link

    @pl.when(t == 1)
    def _():
        turned[...] = link.T

    share = n // S
    link_out[...] = turned[pl.ds(pl.multiple_of(s * share, share), share), :]
    swap.wait_send()
    for d in range(1, R):
        rsp(d).wait_send()
        fan_fin(d).wait_send()
        rsq(d).wait_send()
    for d, e in others:
        fan_l(d, e).wait_send()

    @pl.when(s > 0)
    def _():
        l_half().wait_send()

    @pl.when(s < S - 1)
    def _():
        for d in range(R):
            g_hop(d).wait_send()
            l_hop(d).wait_send()
        for d in range(1, R):
            fan(gout, fout_send, fout_recv, d).wait_send()

    @pl.when(s == S - 1)
    def _():
        for q in range(1, S):
            g_fin(q).wait_send()
            l_fin(q).wait_send()


def chain(block, incoming, S, R):
    modes, n, _ = block.shape
    half = modes // 2
    wide = n // 2
    group = 1
    while group < 4 and half % (2 * group) == 0:
        group *= 2
    blocks = 3 if (3 * wide) % (8 * R) == 0 else 4
    part = blocks * wide // R
    ch = n // R
    dma = pltpu.SemaphoreType.DMA
    vmem = pltpu.VMEM
    packed = vmem((blocks * wide, wide), F32)
    halves = vmem((2, n, wide), F32)
    return pl.pallas_call(
        functools.partial(chain_kernel, S, R, group, blocks),
        out_shape=[jax.ShapeDtypeStruct((3, n, n), F32), jax.ShapeDtypeStruct((n // S, n), F32)],
        in_specs=[pl.BlockSpec(memory_space=pl.ANY), pl.BlockSpec(memory_space=pltpu.VMEM)],
        out_specs=[pl.BlockSpec(memory_space=pltpu.VMEM)] * 2,
        scratch_shapes=[
            vmem((modes, n, n), F32), vmem((half, n, n), F32), vmem((n, n), F32),
            vmem((modes, n, n), BF16), vmem((modes, n, n), BF16),
            vmem((modes, n, n), BF16), vmem((modes, n, n), BF16),
            vmem((half, n, n), BF16), vmem((half, n, n), BF16),
            packed, packed, packed, halves, halves, packed, halves,
            vmem((n, wide), F32), vmem((n, wide), F32),
            vmem((R, part, wide), F32), vmem((R, ch, wide), F32),
            vmem((part, wide), F32), vmem((ch, wide), F32), vmem((n, n), F32), vmem((n, n), F32),
            dma((modes // group,)), dma((2,)), dma((2,)),
            dma((R,)), dma((R,)), dma((R,)), dma((R,)), dma, dma, dma, dma,
            dma((R,)), dma((R,)), dma((R,)), dma((R,)),
            dma((R,)), dma((R,)), dma((R,)), dma((R,)), dma((R, 2)), dma((R, 2)),
            dma((S,)), dma((1,)), dma((S,)), dma((1,)),
        ],
        compiler_params=pltpu.CompilerParams(
            collective_id=0, has_side_effects=True, vmem_limit_bytes=60 * 1024 * 1024
        ),
        name="gram_chain",
    )(block, incoming)


def lower_part(e):
    row = lax.broadcasted_iota(jnp.int32, e.shape, 0)
    col = lax.broadcasted_iota(jnp.int32, e.shape, 1)
    return jnp.where(row > col, e, jnp.where(row == col, 0.5 * e, 0.0))


def frame_kernel(
    group, scale, g_ref, incoming_ref, blocks_ref, frames_ref, tail_ref, x_ref, a_ref, b_ref, u_hi, u_lo, x_hi, x_lo
):
    n = incoming_ref.shape[0]
    count = g_ref.shape[0]
    section = lax.axis_index("cores")

    @pl.when(pl.program_id(0) == 0)
    def _():
        row = lax.broadcasted_iota(jnp.int32, (n, n), 0)
        col = lax.broadcasted_iota(jnp.int32, (n, n), 1)
        eye = (row == col).astype(F32)
        for m in range(count):
            diagonal = jnp.sum(g_ref[m] * eye, axis=0, keepdims=True)
            x_ref[m] = eye * lax.rsqrt(diagonal)

        def residual(m):
            x = x_ref[m]
            return x, mm_nt(mm(x, g_ref[m]), x) - eye

        def step(carry):
            k, _ = carry
            distances = []
            for m in range(count):
                x, e = residual(m)
                x_ref[m] = x - mm(lower_part(e), x)
                distances.append(jnp.sum(e * e))
            return k + 1, tuple(distances)

        def away(carry):
            k, distances = carry
            close = functools.reduce(jnp.logical_and, [d < CLOSE for d in distances])
            return (k < NEWTON_STEPS) & jnp.logical_not(close)

        _, distances = lax.while_loop(away, step, (0, (jnp.float32(1.0),) * count))

        for m in range(count):
            smallest = jnp.min(jnp.where(row == col, x_ref[m], 1.0))

            @pl.when(jnp.logical_not((distances[m] < CLOSE) & (smallest > 0.0)))
            def _(m=m):
                a_ref[...] = g_ref[m]
                b_ref[...] = eye

                def column(j, carry):
                    a = a_ref[...]
                    b = b_ref[...]
                    rowj = jnp.sum(jnp.where(row == j, a, 0.0), axis=0, keepdims=True)
                    pivot = jnp.sum(jnp.where((row == j) & (col == j), a, 0.0), keepdims=True)
                    inv = lax.rsqrt(pivot)
                    colj = jnp.sum(jnp.where(col == j, a, 0.0), axis=1, keepdims=True) * inv
                    below = lax.broadcasted_iota(jnp.int32, (n, 1), 0) > j
                    colj = jnp.where(below, colj, 0.0)
                    bj = jnp.sum(jnp.where(row == j, b, 0.0), axis=0, keepdims=True) * inv
                    a_ref[...] = a - colj * (rowj * inv)
                    b_ref[...] = jnp.where(row == j, bj, b) - colj * bj
                    return carry

                lax.fori_loop(0, n, column, 0)
                x_ref[m] = b_ref[...]

        def factor(m):
            return jnp.where(row <= col, mm(x_ref[m], g_ref[m]), 0.0)

        x_ref[2] = factor(2)
        share = tail_ref.shape[0]
        tail_ref[...] = x_ref[2, pl.ds(pl.multiple_of(section * share, share), share), :]
        upper = jnp.where(section == 0, incoming_ref[...], factor(0))
        hi, lo = split(upper)
        u_hi[...] = hi
        u_lo[...] = lo
        hi, lo = split(jnp.where(row >= col, x_ref[1], 0.0).T * scale)
        x_hi[...] = hi
        x_lo[...] = lo

    u3 = left3(u_hi[...], u_lo[...])
    x3 = right3(x_hi[...], x_lo[...])
    mixed = dot(u3, jnp.concatenate([right3(*split(blocks_ref[j])) for j in range(group)], axis=1))
    for j in range(group):
        frames_ref[j] = dot(left3(*split(mixed[:, j * n : (j + 1) * n])), x3)


def make_frames(grams, incoming, block, scale, S):
    modes, n, _ = block.shape
    group = min(4, modes)
    vmem = pltpu.VMEM
    return pl.pallas_call(
        functools.partial(frame_kernel, group, scale),
        grid=(modes // group,),
        out_shape=[jax.ShapeDtypeStruct((modes, n, n), F32), jax.ShapeDtypeStruct((n // S, n), F32)],
        in_specs=[
            pl.BlockSpec((3, n, n), lambda i: (0, 0, 0)),
            pl.BlockSpec((n, n), lambda i: (0, 0)),
            pl.BlockSpec((group, n, n), lambda i: (i, 0, 0)),
        ],
        out_specs=[
            pl.BlockSpec((group, n, n), lambda i: (i, 0, 0)),
            pl.BlockSpec((n // S, n), lambda i: (0, 0)),
        ],
        scratch_shapes=[
            vmem((3, n, n), F32), vmem((n, n), F32), vmem((n, n), F32),
            vmem((n, n), BF16), vmem((n, n), BF16), vmem((n, n), BF16), vmem((n, n), BF16),
        ],
        compiler_params=pltpu.CompilerParams(vmem_limit_bytes=48 * 1024 * 1024),
        name="frames",
    )(grams, incoming, block)


def shards(S, R, T, modes_all, cores, incoming):
    block = cores[0, 0]
    upper_start = incoming[0]
    n = block.shape[-1]
    grams, link_rows = chain(block, upper_start, S, R)
    scale = float(modes_all * n) ** 0.5
    frames, tail_rows = make_frames(grams, upper_start, block, scale, S)
    return frames[None, None], tail_rows[None], link_rows[None]


def solution(mesh):
    S, R, T = (mesh.shape[name] for name in ("cores", "row", "tensor"))
    in_specs = (P("tensor", "cores", "row", None, None), P("tensor", None, None))
    out_specs = (
        P("tensor", "cores", "row", None, None),
        P("tensor", "cores", None),
        P("tensor", "cores", None),
    )

    def whole(cores, incoming):
        body = functools.partial(shards, S, R, T, cores.shape[2])
        return jax.shard_map(body, mesh=mesh, in_specs=in_specs, out_specs=out_specs, check_vma=False)(
            cores, incoming
        )

    return whole
```

```python
import functools

import jax
import jax.numpy as jnp
from jax import lax
from jax.experimental import pallas as pl
from jax.experimental.pallas import tpu as pltpu
from jax.sharding import PartitionSpec as P

MESH = pl.DeviceIdType.MESH
F32 = jnp.float32
BF16 = jnp.bfloat16
NEWTON_STEPS = 16
CLOSE = 1e-6
WARM_STEPS = 2


def split(x):
    hi = x.astype(BF16)
    return hi, (x - hi.astype(F32)).astype(BF16)


def left3(hi, lo):
    return jnp.concatenate([hi, hi, lo], axis=1)


def right3(hi, lo):
    return jnp.concatenate([hi, lo, hi], axis=0)


def right3t(hi, lo):
    return jnp.concatenate([hi, lo, hi], axis=1)


def dot(a, b):
    return jnp.dot(a, b, preferred_element_type=F32)


def dot_nt(a, b):
    return lax.dot_general(a, b, (((1,), (1,)), ((), ())), preferred_element_type=F32)


def mm(a, b):
    return dot(left3(*split(a)), right3(*split(b)))


def mm_nt(a, b):
    return dot_nt(left3(*split(a)), right3t(*split(b)))


def pack(g, blocks):
    h = g.shape[0] // 2
    parts = [g[:h, :h], g[:h, h:], g[h:, h:]]
    if blocks == 4:
        parts.append(g[h:, :h])
    return jnp.concatenate(parts, axis=0)


def unpack(p):
    h = p.shape[1]
    a, b, c = p[:h], p[h : 2 * h], p[2 * h : 3 * h]
    return jnp.concatenate(
        [jnp.concatenate([a, b], axis=1), jnp.concatenate([b.T, c], axis=1)], axis=0
    )


def lower_part(e):
    row = lax.broadcasted_iota(jnp.int32, e.shape, 0)
    col = lax.broadcasted_iota(jnp.int32, e.shape, 1)
    return jnp.where(row > col, e, jnp.where(row == col, 0.5 * e, 0.0))


def first_guess(g, eye):
    dr = lax.rsqrt(jnp.sum(g * eye, axis=0, keepdims=True))
    dc = lax.rsqrt(jnp.sum(g * eye, axis=1, keepdims=True))
    return (eye - lower_part(g * dr * dc - eye)) * dr


def newton(x, g, eye):
    e = mm_nt(mm(x, g), x) - eye
    return x - mm(lower_part(e), x), e


def chain_kernel(
    S, R, group, blocks,
    cores_ref, incoming_ref,
    grams_out, x_out, link_out,
    raw, other, in_other, c_hi, c_lo, ct_hi, ct_lo, o_hi, o_lo,
    gin, gout, gfin, lin, lfin, p_ref, q_ref, q_got, q_sum, rs_p, rs_q, red_p, red_q, acc, turned,
    raw_sem, pair_send, pair_recv,
    rsp_send, rsp_recv, rsq_send, rsq_recv, swap_send, swap_recv, half_send, half_recv,
    hop_send, hop_recv, lhop_send, lhop_recv,
    fout_send, fout_recv, ffin_send, ffin_recv, flin_send, flin_recv,
    gf_send, gf_recv, lf_send, lf_recv,
):
    s = lax.axis_index("cores")
    r = lax.axis_index("row")
    t = lax.axis_index("tensor")
    modes, n, _ = raw.shape
    half = modes // 2
    ch = n // R
    wide = n // 2

    def row_at(d):
        return lax.rem(r + d, R)

    def tens(e):
        return lax.rem(t + e, 2)

    part = blocks * wide // R

    def rows(k):
        return pl.ds(pl.multiple_of(k * ch, ch), ch)

    def parts(k):
        return pl.ds(pl.multiple_of(k * part, part), part)

    def cols(k):
        return pl.ds(pl.multiple_of(k * wide, wide), wide)

    barrier = pltpu.get_barrier_semaphore()
    greeted = 0
    for d in range(R):
        for e in range(2):
            for q in range(S):
                if d == 0 and e == 0 and q == 0:
                    continue
                if q > 0 and e > 0:
                    continue
                pl.semaphore_signal(
                    barrier, inc=1, device_id=(lax.rem(s + q, S), row_at(d), tens(e)), device_id_type=MESH
                )
                greeted += 1
    pl.semaphore_wait(barrier, greeted)

    def remote(src, dst, send, recv, to):
        return pltpu.make_async_remote_copy(
            src_ref=src, dst_ref=dst, send_sem=send, recv_sem=recv, device_id=to, device_id_type=MESH
        )

    partner = (s, r, tens(1))
    give = remote(cores_ref.at[pl.ds((1 - t) * half, half)], other, pair_send.at[0], pair_recv.at[0], partner)
    give_in = remote(incoming_ref, in_other, pair_send.at[1], pair_recv.at[1], partner)
    give_in.start()
    give.start()

    groups = modes // group
    loads = [
        pltpu.make_async_copy(cores_ref.at[pl.ds(k * group, group)], raw.at[pl.ds(k * group, group)], raw_sem.at[k])
        for k in range(groups)
    ]
    for load in loads:
        load.start()
    for k in range(groups):
        loads[k].wait()

        def prep(j, carry, k=k):
            i = k * group + j
            x = raw[i]
            hi, lo = split(x)
            c_hi[i] = hi
            c_lo[i] = lo
            thi, tlo = split(x.T)
            ct_hi[i] = thi
            ct_lo[i] = tlo
            return carry

        lax.fori_loop(0, group, prep, 0)

    def prep_other():
        give.wait()
        give_in.wait()

        def body(j, carry):
            hi, lo = split(other[j])
            o_hi[j] = hi
            o_lo[j] = lo
            return carry

        lax.fori_loop(0, half, body, 0)

    nxt = lax.rem(s + 1, S)

    def g_hop(d):
        return remote(red_p, gin.at[parts(r)], hop_send.at[d], hop_recv.at[d], (nxt, row_at(d), t))

    def l_hop(d):
        return remote(red_q, lin.at[t, rows(r)], lhop_send.at[d], lhop_recv.at[d], (nxt, row_at(d), t))

    def l_half():
        return remote(lin.at[t], lin.at[t], half_send, half_recv, partner)

    pairs = [(d, e) for d in range(R) for e in range(2)]
    others = pairs[1:]

    @pl.when(s == 0)
    def _():
        u = incoming_ref[...]
        gin[...] = pack(mm(u.T, u), blocks)

    @pl.when(s > 0)
    def _():
        prep_other()
        for d in range(R):
            g_hop(d).wait_recv()

    def run(w, hi_ref, lo_ref, first, count):
        w3 = left3(*split(w))
        acc[...] = jnp.zeros_like(acc)

        def body(k, carry):
            lhs = []
            rhs = []
            for j in range(group):
                i = k * group + j
                y = dot(w3, right3(hi_ref[i], lo_ref[i]))
                rhs.append(right3(*split(y)))
                lhs.append(left3(ct_hi[first + i], ct_lo[first + i]))
            acc[...] += dot(jnp.concatenate(lhs, axis=1), jnp.concatenate(rhs, axis=0))
            return carry

        lax.fori_loop(0, count // group, body, 0)

    run(unpack(gin[...]), c_hi, c_lo, 0, modes)
    p_ref[...] = pack(acc[...], blocks)

    def rsp(d):
        return remote(p_ref.at[parts(row_at(d))], rs_p.at[d], rsp_send.at[d], rsp_recv.at[d], (s, row_at(d), t))

    for d in range(1, R):
        rsp(d).start()

    def put(m):
        lin[0] = m[:, :wide]
        lin[1] = m[:, wide:]

    @pl.when(s == 0)
    def _():
        prep_other()
        u = incoming_ref[...]
        v = in_other[...]

        @pl.when(t == 0)
        def _():
            put(mm(u.T, v))

        @pl.when(t == 1)
        def _():
            put(mm(v.T, u))

    @pl.when(s > 0)
    def _():
        for d in range(R):
            l_hop(d).wait_recv()
        l_half().start()
        l_half().wait_recv()

    first = t * half
    link = jnp.concatenate([lin[0], lin[1]], axis=1)

    @pl.when(t == 0)
    def _():
        run(link, o_hi, o_lo, first, half)
        q_ref[0] = acc[:, :wide]
        q_ref[1] = acc[:, wide:]

    @pl.when(t == 1)
    def _():
        run(link.T, o_hi, o_lo, first, half)
        turned[...] = acc[...].T
        q_ref[0] = turned[:, :wide]
        q_ref[1] = turned[:, wide:]

    swap = remote(q_ref.at[1 - t], q_got, swap_send, swap_recv, partner)
    swap.start()

    for d in range(1, R):
        rsp(d).wait_recv()
    total = p_ref[parts(r), :]
    for d in range(1, R):
        total += rs_p[d]
    red_p[...] = total

    def g_fin(q):
        return remote(red_p, gfin.at[parts(r)], gf_send.at[q], gf_recv.at[0], (lax.rem(s + q, S), r, t))

    def fan(buf, send, recv, d):
        return remote(red_p, buf.at[parts(r)], send.at[d], recv.at[d], (s, row_at(d), t))

    def fan_fin(d):
        return remote(gfin.at[parts(r)], gfin.at[parts(r)], ffin_send.at[d], ffin_recv.at[d], (s, row_at(d), t))

    @pl.when(s < S - 1)
    def _():
        for d in range(R):
            g_hop(d).start()

    @pl.when(s == S - 1)
    def _():
        gfin[parts(r), :] = red_p[...]
        for d in range(1, R):
            fan_fin(d).start()
        for q in range(1, S):
            g_fin(q).start()

    swap.wait_recv()
    q_sum[...] = q_ref[t] + q_got[...]

    def rsq(d):
        return remote(q_sum.at[rows(row_at(d))], rs_q.at[d], rsq_send.at[d], rsq_recv.at[d], (s, row_at(d), t))

    for d in range(1, R):
        rsq(d).start()
    for d in range(1, R):
        rsq(d).wait_recv()
    total = q_sum[rows(r), :]
    for d in range(1, R):
        total += rs_q[d]
    red_q[...] = total

    def l_fin(q):
        return remote(red_q, lfin.at[t, rows(r)], lf_send.at[q], lf_recv.at[0], (lax.rem(s + q, S), r, t))

    def fan_l(d, e):
        return remote(
            lfin.at[t, rows(r)], lfin.at[t, rows(r)], flin_send.at[d, e], flin_recv.at[d, e], (s, row_at(d), tens(e))
        )

    @pl.when(s < S - 1)
    def _():
        for d in range(R):
            l_hop(d).start()
        gout[parts(r), :] = red_p[...]
        for d in range(1, R):
            fan(gout, fout_send, fout_recv, d).start()
        g_fin(0).wait_recv()
        for d in range(1, R):
            fan_fin(d).start()
        l_fin(0).wait_recv()

    @pl.when(s == S - 1)
    def _():
        lfin[t, rows(r)] = red_q[...]
        for q in range(1, S):
            l_fin(q).start()

    for d, e in others:
        fan_l(d, e).start()

    for d in range(1, R):
        fan_fin(d).wait_recv()
    final = unpack(gfin[...])
    grams_out[2] = final

    row = lax.broadcasted_iota(jnp.int32, (n, n), 0)
    col = lax.broadcasted_iota(jnp.int32, (n, n), 1)
    eye = (row == col).astype(F32)

    @pl.when(s == 0)
    def _():
        grams_out[0] = eye

    @pl.when(s > 0)
    def _():
        grams_out[0] = unpack(gin[...])

    @pl.when(s < S - 1)
    def _():
        for d in range(1, R):
            fan(gout, fout_send, fout_recv, d).wait_recv()
        grams_out[1] = unpack(gout[...])

    @pl.when(s == S - 1)
    def _():
        grams_out[1] = final

    for m in range(3):
        x_out[m] = first_guess(grams_out[m], eye)

    def warm(k, carry):
        new = [newton(x_out[m], grams_out[m], eye)[0] for m in range(3)]
        for m in range(3):
            x_out[m] = new[m]
        return carry

    lax.fori_loop(0, WARM_STEPS, warm, 0)

    for d, e in others:
        fan_l(d, e).wait_recv()
    link = jnp.concatenate([lfin[0], lfin[1]], axis=1)

    @pl.when(t == 0)
    def _():
        turned[...] = link

    @pl.when(t == 1)
    def _():
        turned[...] = link.T

    share = n // S
    link_out[...] = turned[pl.ds(pl.multiple_of(s * share, share), share), :]
    swap.wait_send()
    for d in range(1, R):
        rsp(d).wait_send()
        fan_fin(d).wait_send()
        rsq(d).wait_send()
    for d, e in others:
        fan_l(d, e).wait_send()

    @pl.when(s > 0)
    def _():
        l_half().wait_send()

    @pl.when(s < S - 1)
    def _():
        for d in range(R):
            g_hop(d).wait_send()
            l_hop(d).wait_send()
        for d in range(1, R):
            fan(gout, fout_send, fout_recv, d).wait_send()

    @pl.when(s == S - 1)
    def _():
        for q in range(1, S):
            g_fin(q).wait_send()
            l_fin(q).wait_send()


def chain(block, incoming, S, R):
    modes, n, _ = block.shape
    half = modes // 2
    wide = n // 2
    group = 1
    while group < 4 and half % (2 * group) == 0:
        group *= 2
    blocks = 3 if (3 * wide) % (8 * R) == 0 else 4
    part = blocks * wide // R
    ch = n // R
    dma = pltpu.SemaphoreType.DMA
    vmem = pltpu.VMEM
    packed = vmem((blocks * wide, wide), F32)
    halves = vmem((2, n, wide), F32)
    return pl.pallas_call(
        functools.partial(chain_kernel, S, R, group, blocks),
        out_shape=[jax.ShapeDtypeStruct((3, n, n), F32)] * 2 + [jax.ShapeDtypeStruct((n // S, n), F32)],
        in_specs=[pl.BlockSpec(memory_space=pl.ANY), pl.BlockSpec(memory_space=pltpu.VMEM)],
        out_specs=[pl.BlockSpec(memory_space=pltpu.VMEM)] * 3,
        scratch_shapes=[
            vmem((modes, n, n), F32), vmem((half, n, n), F32), vmem((n, n), F32),
            vmem((modes, n, n), BF16), vmem((modes, n, n), BF16),
            vmem((modes, n, n), BF16), vmem((modes, n, n), BF16),
            vmem((half, n, n), BF16), vmem((half, n, n), BF16),
            packed, packed, packed, halves, halves, packed, halves,
            vmem((n, wide), F32), vmem((n, wide), F32),
            vmem((R, part, wide), F32), vmem((R, ch, wide), F32),
            vmem((part, wide), F32), vmem((ch, wide), F32), vmem((n, n), F32), vmem((n, n), F32),
            dma((modes // group,)), dma((2,)), dma((2,)),
            dma((R,)), dma((R,)), dma((R,)), dma((R,)), dma, dma, dma, dma,
            dma((R,)), dma((R,)), dma((R,)), dma((R,)),
            dma((R,)), dma((R,)), dma((R,)), dma((R,)), dma((R, 2)), dma((R, 2)),
            dma((S,)), dma((1,)), dma((S,)), dma((1,)),
        ],
        compiler_params=pltpu.CompilerParams(
            collective_id=0, has_side_effects=True, vmem_limit_bytes=60 * 1024 * 1024
        ),
        name="gram_chain",
    )(block, incoming)


def frame_kernel(
    group, scale, g_ref, start_ref, incoming_ref, blocks_ref, frames_ref, tail_ref, x_ref, a_ref, b_ref, u_hi, u_lo, x_hi, x_lo
):
    n = incoming_ref.shape[0]
    count = g_ref.shape[0]
    section = lax.axis_index("cores")

    @pl.when(pl.program_id(0) == 0)
    def _():
        row = lax.broadcasted_iota(jnp.int32, (n, n), 0)
        col = lax.broadcasted_iota(jnp.int32, (n, n), 1)
        eye = (row == col).astype(F32)
        x_ref[...] = start_ref[...]

        def step(carry):
            k, _ = carry
            new = [newton(x_ref[m], g_ref[m], eye) for m in range(count)]
            distances = []
            for m, (x, e) in enumerate(new):
                x_ref[m] = x
                distances.append(jnp.sum(e * e))
            return k + 1, tuple(distances)

        def away(carry):
            k, distances = carry
            close = functools.reduce(jnp.logical_and, [d < CLOSE for d in distances])
            return (k < NEWTON_STEPS) & jnp.logical_not(close)

        _, distances = lax.while_loop(away, step, (0, (jnp.float32(1.0),) * count))

        for m in range(count):
            smallest = jnp.min(jnp.where(row == col, x_ref[m], 1.0))

            @pl.when(jnp.logical_not((distances[m] < CLOSE) & (smallest > 0.0)))
            def _(m=m):
                a_ref[...] = g_ref[m]
                b_ref[...] = eye

                def column(j, carry):
                    a = a_ref[...]
                    b = b_ref[...]
                    rowj = jnp.sum(jnp.where(row == j, a, 0.0), axis=0, keepdims=True)
                    pivot = jnp.sum(jnp.where((row == j) & (col == j), a, 0.0), keepdims=True)
                    inv = lax.rsqrt(pivot)
                    colj = jnp.sum(jnp.where(col == j, a, 0.0), axis=1, keepdims=True) * inv
                    below = lax.broadcasted_iota(jnp.int32, (n, 1), 0) > j
                    colj = jnp.where(below, colj, 0.0)
                    bj = jnp.sum(jnp.where(row == j, b, 0.0), axis=0, keepdims=True) * inv
                    a_ref[...] = a - colj * (rowj * inv)
                    b_ref[...] = jnp.where(row == j, bj, b) - colj * bj
                    return carry

                lax.fori_loop(0, n, column, 0)
                x_ref[m] = b_ref[...]

        def factor(m):
            return jnp.where(row <= col, mm(x_ref[m], g_ref[m]), 0.0)

        x_ref[2] = factor(2)
        share = tail_ref.shape[0]
        tail_ref[...] = x_ref[2, pl.ds(pl.multiple_of(section * share, share), share), :]
        upper = jnp.where(section == 0, incoming_ref[...], factor(0))
        hi, lo = split(upper)
        u_hi[...] = hi
        u_lo[...] = lo
        hi, lo = split(jnp.where(row >= col, x_ref[1], 0.0).T * scale)
        x_hi[...] = hi
        x_lo[...] = lo

    u3 = left3(u_hi[...], u_lo[...])
    x3 = right3(x_hi[...], x_lo[...])
    mixed = dot(u3, jnp.concatenate([right3(*split(blocks_ref[j])) for j in range(group)], axis=1))
    for j in range(group):
        frames_ref[j] = dot(left3(*split(mixed[:, j * n : (j + 1) * n])), x3)


def make_frames(grams, start, incoming, block, scale, S):
    modes, n, _ = block.shape
    group = min(4, modes)
    vmem = pltpu.VMEM
    return pl.pallas_call(
        functools.partial(frame_kernel, group, scale),
        grid=(modes // group,),
        out_shape=[jax.ShapeDtypeStruct((modes, n, n), F32), jax.ShapeDtypeStruct((n // S, n), F32)],
        in_specs=[
            pl.BlockSpec((3, n, n), lambda i: (0, 0, 0)),
            pl.BlockSpec((3, n, n), lambda i: (0, 0, 0)),
            pl.BlockSpec((n, n), lambda i: (0, 0)),
            pl.BlockSpec((group, n, n), lambda i: (i, 0, 0)),
        ],
        out_specs=[
            pl.BlockSpec((group, n, n), lambda i: (i, 0, 0)),
            pl.BlockSpec((n // S, n), lambda i: (0, 0)),
        ],
        scratch_shapes=[
            vmem((3, n, n), F32), vmem((n, n), F32), vmem((n, n), F32),
            vmem((n, n), BF16), vmem((n, n), BF16), vmem((n, n), BF16), vmem((n, n), BF16),
        ],
        compiler_params=pltpu.CompilerParams(vmem_limit_bytes=48 * 1024 * 1024),
        name="frames",
    )(grams, start, incoming, block)


def shards(S, R, T, modes_all, cores, incoming):
    block = cores[0, 0]
    upper_start = incoming[0]
    n = block.shape[-1]
    grams, start, link_rows = chain(block, upper_start, S, R)
    scale = float(modes_all * n) ** 0.5
    frames, tail_rows = make_frames(grams, start, upper_start, block, scale, S)
    return frames[None, None], tail_rows[None], link_rows[None]


def solution(mesh):
    S, R, T = (mesh.shape[name] for name in ("cores", "row", "tensor"))
    in_specs = (P("tensor", "cores", "row", None, None), P("tensor", None, None))
    out_specs = (
        P("tensor", "cores", "row", None, None),
        P("tensor", "cores", None),
        P("tensor", "cores", None),
    )

    def whole(cores, incoming):
        body = functools.partial(shards, S, R, T, cores.shape[2])
        return jax.shard_map(body, mesh=mesh, in_specs=in_specs, out_specs=out_specs, check_vma=False)(
            cores, incoming
        )

    return whole
```
